32 devices in a mesh: groups: 2 (over x), vocab: 8 (over z, y), tok: 2 (over core).
Axes of the slice: x: 2, y: 2, z: 4, core: 2. Of those that a mesh axis runs over, the one named last changes fastest.
Arguments:
- teacher_hidden: bfloat16 [1024, 8192], P(('groups', 'tok'), 'vocab'), parts along dimension 0
- teacher_weight: bfloat16 [8192, 76032], P(None, ('vocab', 'tok')), may hold values from -0.1875 to 0.1875
- student_hidden: bfloat16 [1024, 2048], P(('groups', 'tok'), 'vocab'), parts along dimension 0
- student_weight: bfloat16 [2048, 76032], P(None, ('vocab', 'tok')), may hold values from -0.375 to 0.375
- loss_mask: int32 [1024], P(('groups', 'tok')), parts along dimension 0, may hold values 0 or 1
Outputs:
- kl_token: float32 [1024], P(('groups', 'tok')), parts along dimension 0
- grad_hidden: bfloat16 [1024, 2048], P(('groups', 'tok'), 'vocab'), parts along dimension 0
The draws below stay inside these ranges and needn't reach their ends.
There are 2 independent parts, one for each index of `groups`. The reference program is written for one: setup_inputs(seed, part) draws one part's arguments, and reference() takes and returns one part's arrays. A program takes and returns all parts, laid end to end along the dimension named above; an argument that names none is the same for every part. Nothing has to cross between parts.
All inputs are finite; a program needn't handle non-finite values. No bound on the sum of `loss_mask` on one device may be relied on, other than what follows from the above.
Results may differ from the reference program's by a relative error of at most 0.0049.
Values may be sent and summed in bfloat16 or wider, within the bound.
No kernel may reach another device: no remote copies, remote signals or barrier semaphores. Data moves between devices by JAX's collectives and lax.ppermute only.
A program may use at most 576 MiB of HBM per device.

```python
import jax
import jax.numpy as jnp

DT = 8192
DS = 2048
V = 76032
TOKENS = 512


def hidden_rows(key, rows, columns):
    first_key = jax.random.fold_in(key, 0)
    base_values = jax.random.normal(first_key, (rows, columns), jnp.float32)
    return jnp.clip(base_values, -6.0, 6.0).astype(jnp.bfloat16)


def draw_teacher_hidden(key, part):
    return hidden_rows(jax.random.fold_in(key, 11), TOKENS, DT)


def draw_student_hidden(key, part):
    return hidden_rows(jax.random.fold_in(key, 23), TOKENS, DS)


def set_ends(drawn, own_key, least, top_value):
    longest = drawn.shape.index(max(drawn.shape))
    spots = []
    for shift in (0, 1):
        where = [jax.random.randint(jax.random.fold_in(own_key, axis), (), 0, length) for axis, length in enumerate(drawn.shape)]
        where[longest] = (where[longest] + shift) % drawn.shape[longest]
        spots.append(tuple(where))
    return drawn.at[spots[0]].set(least).at[spots[1]].set(top_value)


def block_levels(own_key, extent, cuts, low, top_value):
    def one(axis_at, blocks):
        draws = jax.random.uniform(jax.random.fold_in(jax.random.fold_in(own_key, 6), axis_at), (blocks,), jnp.float32, low / len(cuts), top_value / len(cuts))
        return jnp.repeat(jnp.exp(draws), extent[axis_at] // blocks).reshape((-1,) + (1,) * (len(extent) - axis_at - 1))

    loudness = one(*cuts[0])
    for cut in cuts[1:]:
        loudness = loudness * one(*cut)
    return loudness


def scatter_about(rng, dims, deviation, reach, cuts=(), held_as=jnp.bfloat16):
    values = jax.random.normal(rng, dims, jnp.float32) * deviation
    if len(cuts) > 0:
        values = block_levels(rng, dims, cuts, -0.22, 0.18) * values
    return jnp.clip(values, min=-reach, max=reach).astype(held_as)


def setup_inputs(seed: int = 0, part: int = 0) -> dict:
    streams_of = jax.random.split(jax.random.key(seed), 6)
    own_keys = jax.random.split(jax.random.fold_in(streams_of[5], part), 6)
    teacher_hidden = draw_teacher_hidden(jax.random.fold_in(jax.random.fold_in(streams_of[5], part), 71), part)
    teacher_weight = scatter_about(streams_of[1], (DT, V), (DT // 9) ** -0.5, 0.1875, ((1, 16),))
    student_hidden = draw_student_hidden(jax.random.fold_in(jax.random.fold_in(streams_of[5], part), 71), part)
    student_weight = scatter_about(streams_of[3], (DS, V), (DS // 9) ** -0.5, 0.375, ((1, 16),))
    loss_mask = set_ends((jax.random.randint(own_keys[4], (TOKENS,), 0, 4) < 3).astype(jnp.int32), jax.random.fold_in(own_keys[4], 1), 0, 1)
    return dict(teacher_hidden=teacher_hidden, teacher_weight=teacher_weight, student_hidden=student_hidden, student_weight=student_weight, loss_mask=loss_mask)


loss_scale = 16.0


def reference(teacher_hidden, teacher_weight, student_hidden, student_weight, loss_mask):
    teacher_logits = jnp.dot(teacher_hidden, teacher_weight, preferred_element_type=jnp.float32)
    teacher_logp = teacher_logits - jax.nn.logsumexp(teacher_logits, axis=1, keepdims=True)
    student_logits = jnp.dot(student_hidden, student_weight, preferred_element_type=jnp.float32)
    student_lse = jax.nn.logsumexp(student_logits, axis=1)
    teacher_prob = jnp.exp(teacher_logp)
    kl_token = jnp.sum(teacher_prob * (teacher_logp - student_logits), axis=1) + student_lse
    student_prob = jnp.exp(student_logits - student_lse[:, None])
    mask_rows = loss_scale * loss_mask.astype(jnp.float32)
    grad_logits = (mask_rows[:, None] * (student_prob - teacher_prob)).astype(jnp.bfloat16)
    grad_hidden = jnp.dot(grad_logits, student_weight.T, preferred_element_type=jnp.float32)
    return kl_token, grad_hidden.astype(jnp.bfloat16)
```

```python
import functools

import jax
import jax.numpy as jnp
from jax import lax
from jax.experimental import pallas as pl
from jax.experimental.pallas import tpu as pltpu
from jax.sharding import PartitionSpec as P

loss_scale = 16.0
f32 = jnp.float32
bf16 = jnp.bfloat16
MIB = 1 << 20
NT = (((1,), (1,)), ((), ()))
TN = (((0,), (0,)), ((), ()))
WHOLE = pl.BlockSpec(memory_space=pltpu.VMEM)
SWAP = ((0, 1), (1, 0))


def rows_per_block(rows, cap):
    for count in range(1, rows // 16 + 1):
        if rows % (16 * count) == 0 and rows // count <= cap:
            return rows // count
    return rows


def pinned(array):
    return pltpu.with_memory_space_constraint(array, pltpu.VMEM)


def stage_kernel(picks, pieces, dt, first, last, block, off_ref, *refs):
    refs = list(refs)
    shards = len(picks)

    def take(count):
        taken = refs[:count]
        del refs[:count]
        return taken

    parts = take(shards * pieces)
    wt, ws = take(shards), take(shards)
    held = None if first else take(2)
    t_out, s_out = take(2)
    stats = take(1)[0] if last else None
    xt, xs = take(2)
    run = take(1)[0] if last else None
    step = pl.program_id(0)

    @pl.when(step == 0)
    def _():
        for shard in range(shards):
            at = 0
            for part in parts[shard * pieces : (shard + 1) * pieces]:
                span = pl.ds(at, part.shape[0])
                xt[shard, span, :] = part[:, :dt]
                xs[shard, span, :] = part[:, dt:]
                at += part.shape[0]
        if last:
            run[...] = jnp.zeros_like(run)
            run[0:1, :] = jnp.full((1, run.shape[1]), -jnp.inf, f32)
            run[3:4, :] = jnp.full((1, run.shape[1]), -jnp.inf, f32)

    here = pl.ds(pl.multiple_of(step * block, 16), block)
    t = s = None
    for shard in range(shards):
        t_add = lax.dot_general(wt[shard][...], xt[shard], NT, preferred_element_type=f32)
        s_add = lax.dot_general(ws[shard][...], xs[shard], NT, preferred_element_type=f32)
        t = t_add if t is None else t + t_add
        s = s_add if s is None else s + s_add
    if not first:
        t = t + held[0][here, :]
        s = s + held[1][here, :]
    t_out[here, :] = t
    s_out[here, :] = s
    if last:
        t_top = jnp.maximum(run[0:1, :], jnp.max(t, axis=0, keepdims=True))
        s_top = jnp.maximum(run[3:4, :], jnp.max(s, axis=0, keepdims=True))
        t_exp = jnp.exp(t - t_top)
        t_fade = jnp.exp(run[0:1, :] - t_top)
        s_fade = jnp.exp(run[3:4, :] - s_top)
        run[1:2, :] = run[1:2, :] * t_fade + jnp.sum(t_exp, axis=0, keepdims=True)
        run[2:3, :] = run[2:3, :] * t_fade + jnp.sum(t_exp * (t - s), axis=0, keepdims=True)
        run[4:5, :] = run[4:5, :] * s_fade + jnp.sum(jnp.exp(s - s_top), axis=0, keepdims=True)
        run[0:1, :] = t_top
        run[3:4, :] = s_top

        @pl.when(step == pl.num_programs(0) - 1)
        def _():
            stats[...] = run[...]


def stage(shards, picks, offs, wt, ws, held, dt, ds, last):
    count, pieces = len(shards), len(shards[0])
    vocab = wt.shape[0]
    rows = sum(part.shape[0] for part in shards[0])
    block = rows_per_block(vocab, 800)
    parts = [part for shard in shards for part in shard]
    in_specs = [
        pl.BlockSpec(part.shape, lambda j, o: (0, 0), pipeline_mode=pl.Buffered(1))
        for part in parts
    ]
    for width in (dt, ds):
        in_specs += [
            pl.BlockSpec((block, width), lambda j, o, pick=pick: (j, o[pick])) for pick in picks
        ]
    args = parts + [wt] * count + [ws] * count
    aliases = {}
    if held is not None:
        aliases = {1 + len(args): 0, 2 + len(args): 1}
        in_specs += [WHOLE, WHOLE]
        args += [pinned(array) for array in held]
    logits = pltpu.VMEM((vocab, rows), f32)
    out_shape, out_specs = [logits, logits], [WHOLE, WHOLE]
    scratch = [pltpu.VMEM((count, rows, dt), bf16), pltpu.VMEM((count, rows, ds), bf16)]
    if last:
        out_shape.append(jax.ShapeDtypeStruct((8, rows), f32))
        out_specs.append(pl.BlockSpec((8, rows), lambda j, o: (0, 0)))
        scratch.append(pltpu.VMEM((8, rows), f32))
    return pl.pallas_call(
        functools.partial(stage_kernel, picks, pieces, dt, held is None, last, block),
        grid_spec=pltpu.PrefetchScalarGridSpec(
            num_scalar_prefetch=1,
            grid=(vocab // block,),
            in_specs=in_specs,
            out_specs=out_specs,
            scratch_shapes=scratch,
        ),
        out_shape=out_shape,
        input_output_aliases=aliases,
        compiler_params=pltpu.CompilerParams(vmem_limit_bytes=30 * MIB),
        cost_estimate=pl.CostEstimate(
            flops=2 * rows * count * (dt + ds) * vocab,
            bytes_accessed=2 * count * (dt + ds) * vocab,
            transcendentals=2 * rows * vocab if last else 0,
        ),
        name="stage_last" if last else "stage",
    )(offs, *args)


def grad_kernel(block, stats, t_ref, s_ref, ws, kl, own, other, total, lse):
    step = pl.program_id(0)
    rows = t_ref.shape[1]
    half = rows // 2

    @pl.when(step == 0)
    def _():
        sides = []
        for source in range(stats.shape[0]):
            both = stats[source]
            sides.append(both[:8])
            sides.append(jnp.concatenate([both[8:, half:], both[8:, :half]], axis=1))
        t_top = functools.reduce(jnp.maximum, [side[0:1] for side in sides])
        s_top = functools.reduce(jnp.maximum, [side[3:4] for side in sides])
        t_sum = sum(side[1:2] * jnp.exp(side[0:1] - t_top) for side in sides)
        cross = sum(side[2:3] * jnp.exp(side[0:1] - t_top) for side in sides)
        s_sum = sum(side[4:5] * jnp.exp(side[3:4] - s_top) for side in sides)
        t_lse = t_top + jnp.log(t_sum)
        s_lse = s_top + jnp.log(s_sum)
        lse[0:1, :] = t_lse
        lse[1:2, :] = s_lse
        kl[...] = cross / t_sum - t_lse + s_lse
        total[...] = jnp.zeros_like(total)

    here = pl.ds(pl.multiple_of(step * block, 16), block)
    student = jnp.exp(s_ref[here, :] - lse[1:2, :])
    teacher = jnp.exp(t_ref[here, :] - lse[0:1, :])
    grad = (student - teacher).astype(bf16)
    total[...] += lax.dot_general(grad, ws[...], TN, preferred_element_type=f32)

    @pl.when(step == pl.num_programs(0) - 1)
    def _():
        width = own.shape[2]
        for dest in range(own.shape[0]):
            own[dest] = total[:half, dest * width : (dest + 1) * width]
            other[dest] = total[half:, dest * width : (dest + 1) * width].astype(bf16)


def grad_partial(stats, t, s, ws, count):
    vocab, rows = t.shape
    features = ws.shape[1]
    block = rows_per_block(vocab, 800)
    half, width = rows // 2, features // count
    return pl.pallas_call(
        functools.partial(grad_kernel, block),
        grid=(vocab // block,),
        in_specs=[
            pl.BlockSpec(stats.shape, lambda j: (0, 0, 0), pipeline_mode=pl.Buffered(1)),
            WHOLE,
            WHOLE,
            pl.BlockSpec((block, features), lambda j: (j, 0)),
        ],
        out_specs=[
            pl.BlockSpec((1, rows), lambda j: (0, 0)),
            pl.BlockSpec((count, half, width), lambda j: (0, 0, 0)),
            pl.BlockSpec((count, half, width), lambda j: (0, 0, 0)),
        ],
        out_shape=[
            jax.ShapeDtypeStruct((1, rows), f32),
            jax.ShapeDtypeStruct((count, half, width), f32),
            jax.ShapeDtypeStruct((count, half, width), bf16),
        ],
        scratch_shapes=[pltpu.VMEM((rows, features), f32), pltpu.VMEM((8, rows), f32)],
        compiler_params=pltpu.CompilerParams(vmem_limit_bytes=30 * MIB),
        cost_estimate=pl.CostEstimate(
            flops=2 * rows * features * vocab,
            bytes_accessed=2 * features * vocab,
            transcendentals=2 * rows * vocab,
        ),
        name="grad",
    )(stats, pinned(t), pinned(s), ws)


def ring_order(count):
    return list(range(0, count, 2)) + list(range(count - 1, 0, -2))


def ringed(teacher_hidden, teacher_weight, student_hidden, student_weight, loss_mask):
    count = lax.axis_size("vocab")
    dt, ds = teacher_hidden.shape[1], student_hidden.shape[1]
    order = ring_order(count)
    place = {device: at for at, device in enumerate(order)}
    table = [[order[(place[d] + k) % count] for k in range(count)] for d in range(count)]
    offs = lax.dynamic_index_in_dim(
        jnp.array(table, jnp.int32), lax.axis_index("vocab"), 0, False
    )
    up = [(order[i], order[(i + 1) % count]) for i in range(count)]
    down = [(b, a) for a, b in up]

    def sibling(array):
        return lax.ppermute(array, "tok", SWAP)

    mine = jnp.concatenate([teacher_hidden, student_hidden], axis=1)
    half = mine.shape[0] // 2
    wt, ws = teacher_weight.T, student_weight.T
    from_low = from_high = mine
    held = stage([(mine, sibling(mine))], (0,), offs, wt, ws, None, dt, ds, count == 1)
    for hop in range(1, count // 2 + 1):
        if hop < count // 2:
            from_low = lax.ppermute(from_low, "vocab", up)
            from_high = lax.ppermute(from_high, "vocab", down)
            shards = [
                (from_low, sibling(from_low)),
                (from_high, sibling(from_high)),
            ]
            picks = (count - hop, hop)
        else:
            from_low = lax.ppermute(from_low[:half], "vocab", up)
            from_high = lax.ppermute(from_high[half:], "vocab", down)
            shards = [(from_low, from_high, sibling(from_low), sibling(from_high))]
            picks = (hop,)
        held = stage(shards, picks, offs, wt, ws, held, dt, ds, hop == count // 2)
    t, s, stats = held
    both = jnp.concatenate([stats, sibling(stats)], axis=0)
    every = lax.all_to_all(
        jnp.broadcast_to(both[None], (count,) + both.shape), "vocab", 0, 0, tiled=True
    )
    kl, own, other = grad_partial(every, t, s, ws, count)
    rows = teacher_hidden.shape[0]
    partial = (own + sibling(other).astype(f32)).astype(bf16)
    shares = lax.all_to_all(partial, "vocab", 0, 0, tiled=True)
    mask = loss_scale * loss_mask.astype(f32)
    grad = mask[:, None] * jnp.sum(shares.astype(f32), axis=0)
    return (kl[0, :rows], grad.astype(bf16))


def gathered(teacher_hidden, teacher_weight, student_hidden, student_weight, loss_mask):
    axes = ("vocab", "tok")

    def every_row(hidden):
        own = lax.all_gather(hidden, "vocab", axis=1, tiled=True)
        return lax.all_gather(own, "tok", axis=0, tiled=True)

    t = jnp.dot(every_row(teacher_hidden), teacher_weight, preferred_element_type=f32)
    s = jnp.dot(every_row(student_hidden), student_weight, preferred_element_type=f32)

    def log_total(logits):
        top = lax.pmax(jnp.max(logits, axis=1), axes)
        return top + jnp.log(lax.psum(jnp.sum(jnp.exp(logits - top[:, None]), axis=1), axes))

    t_log = t - log_total(t)[:, None]
    s_log = s - log_total(s)[:, None]
    teacher = jnp.exp(t_log)
    kl = lax.psum(jnp.sum(teacher * (t_log - s_log), axis=1), axes)
    grad = (jnp.exp(s_log) - teacher).astype(bf16)
    part = lax.dot_general(grad, student_weight, NT, preferred_element_type=f32)
    part = lax.psum_scatter(part, "tok", scatter_dimension=0, tiled=True)
    part = lax.psum_scatter(part, "vocab", scatter_dimension=1, tiled=True)
    rows = teacher_hidden.shape[0]
    mask = loss_scale * loss_mask.astype(f32)
    kl = lax.dynamic_slice_in_dim(kl, lax.axis_index("tok") * rows, rows)
    return (kl, (mask[:, None] * part).astype(bf16))


def shards(teacher_hidden, teacher_weight, student_hidden, student_weight, loss_mask):
    count = lax.axis_size("vocab")
    lanes = teacher_hidden.shape[1] % 128 == 0 and student_hidden.shape[1] % 128 == 0
    rows = teacher_hidden.shape[0] % 32 == 0 and teacher_weight.shape[1] % 16 == 0
    fits = lanes and rows and count % 2 == 0 and lax.axis_size("tok") == 2
    run = ringed if fits else gathered
    return run(teacher_hidden, teacher_weight, student_hidden, student_weight, loss_mask)


def solution(mesh):
    return jax.shard_map(
        shards,
        mesh=mesh,
        in_specs=(
            P(("groups", "tok"), "vocab"),
            P(None, ("vocab", "tok")),
            P(("groups", "tok"), "vocab"),
            P(None, ("vocab", "tok")),
            P(("groups", "tok")),
        ),
        out_specs=(P(("groups", "tok")), P(("groups", "tok"), "vocab")),
        check_vma=False,
    )
```

```python
import functools

import jax
import jax.numpy as jnp
from jax import lax
from jax.experimental import pallas as pl
from jax.experimental.pallas import tpu as pltpu
from jax.sharding import PartitionSpec as P

loss_scale = 16.0
f32 = jnp.float32
bf16 = jnp.bfloat16
MIB = 1 << 20
last_block = 1024
NT = (((1,), (1,)), ((), ()))
TN = (((0,), (0,)), ((), ()))
WHOLE = pl.BlockSpec(memory_space=pltpu.VMEM)
SWAP = ((0, 1), (1, 0))


def rows_per_block(rows, cap):
    for count in range(1, rows // 8 + 1):
        if rows % (8 * count) == 0 and rows // count <= cap:
            return rows // count
    return rows


def pinned(array):
    return pltpu.with_memory_space_constraint(array, pltpu.VMEM)


def stage_kernel(count, pieces, dt, first, block, off_ref, *refs):
    refs = list(refs)

    def take(number):
        taken = refs[:number]
        del refs[:number]
        return taken

    parts = take(count * pieces)
    wt, ws = take(count), take(count)
    held = None if first else take(2)
    t_out, s_out = take(2)
    tops, stats = take(2) if len(refs) > 2 else (None, None)
    xt, xs = take(2)
    run = take(1)[0] if tops is not None else None
    step, steps = pl.program_id(0), pl.num_programs(0)
    vocab, rows = t_out.shape

    @pl.when(step == 0)
    def _():
        for shard in range(count):
            at = 0
            for part in parts[shard * pieces : (shard + 1) * pieces]:
                span = pl.ds(at, part.shape[0])
                xt[shard, span, :] = part[:, :dt]
                xs[shard, span, :] = part[:, dt:]
                at += part.shape[0]
        if run is not None:
            run[...] = jnp.zeros_like(run)
            run[0:1, :] = jnp.full((1, rows), -jnp.inf, f32)
            run[3:4, :] = jnp.full((1, rows), -jnp.inf, f32)

    def multiply(size):
        here = pl.ds(pl.multiple_of(step * block, 8), size)
        t = s = None
        for shard in range(count):
            t_add = lax.dot_general(wt[shard][:size], xt[shard], NT, preferred_element_type=f32)
            s_add = lax.dot_general(ws[shard][:size], xs[shard], NT, preferred_element_type=f32)
            t = t_add if t is None else t + t_add
            s = s_add if s is None else s + s_add
        if not first:
            t = t + held[0][here, :]
            s = s + held[1][here, :]
        if run is None:
            t_out[here, :] = t
            s_out[here, :] = s
            return
        t_top = jnp.max(t, axis=0, keepdims=True)
        s_top = jnp.max(s, axis=0, keepdims=True)
        t_exp = jnp.exp(t - t_top)
        s_exp = jnp.exp(s - s_top)
        t_out[here, :] = t_exp
        s_out[here, :] = s_exp
        tops[step, 0:1, :] = t_top
        tops[step, 1:2, :] = s_top
        t_new = jnp.maximum(run[0:1, :], t_top)
        s_new = jnp.maximum(run[3:4, :], s_top)
        t_old, t_add = jnp.exp(run[0:1, :] - t_new), jnp.exp(t_top - t_new)
        s_old, s_add = jnp.exp(run[3:4, :] - s_new), jnp.exp(s_top - s_new)
        t_sum = jnp.sum(t_exp, axis=0, keepdims=True)
        cross = jnp.sum(t_exp * (t - s), axis=0, keepdims=True)
        s_sum = jnp.sum(s_exp, axis=0, keepdims=True)
        run[1:2, :] = run[1:2, :] * t_old + t_sum * t_add
        run[2:3, :] = run[2:3, :] * t_old + cross * t_add
        run[4:5, :] = run[4:5, :] * s_old + s_sum * s_add
        run[0:1, :] = t_new
        run[3:4, :] = s_new

    by_block(step, vocab, block, multiply)
    if run is not None:

        @pl.when(step == steps - 1)
        def _():
            for dest in range(stats.shape[0]):
                stats[dest] = run[...]


def by_block(step, vocab, block, body):
    whole, tail = vocab // block, vocab % block
    if tail == 0:
        body(block)
        return
    if whole > 0:
        pl.when(step < whole)(functools.partial(body, block))
    pl.when(step == whole)(functools.partial(body, tail))


def stage(shards, picks, offs, wt, ws, held, dt, ds, copies=0):
    count, pieces = len(shards), len(shards[0])
    vocab = wt.shape[0]
    last = copies > 0
    rows = sum(part.shape[0] for part in shards[0])
    block = last_block if last else rows_per_block(vocab, 800)
    block = min(block, vocab)
    blocks = pl.cdiv(vocab, block)
    parts = [part for shard in shards for part in shard]
    in_specs = [
        pl.BlockSpec(part.shape, lambda j, o: (0, 0), pipeline_mode=pl.Buffered(1))
        for part in parts
    ]
    for width in (dt, ds):
        in_specs += [
            pl.BlockSpec((block, width), lambda j, o, pick=pick: (j, o[pick])) for pick in picks
        ]
    args = parts + [wt] * count + [ws] * count
    aliases = {}
    if held is not None:
        aliases = {1 + len(args): 0, 2 + len(args): 1}
        in_specs += [WHOLE, WHOLE]
        args += [pinned(array) for array in held]
    out_shape, out_specs = [pltpu.VMEM((vocab, rows), f32)] * 2, [WHOLE, WHOLE]
    scratch = [pltpu.VMEM((count, rows, dt), bf16), pltpu.VMEM((count, rows, ds), bf16)]
    if last:
        for shape in ((blocks, 8, rows), (copies, 8, rows)):
            out_shape.append(jax.ShapeDtypeStruct(shape, f32))
            out_specs.append(pl.BlockSpec(shape, lambda j, o: (0, 0, 0)))
        scratch.append(pltpu.VMEM((8, rows), f32))
    return pl.pallas_call(
        functools.partial(stage_kernel, count, pieces, dt, held is None, block),
        grid_spec=pltpu.PrefetchScalarGridSpec(
            num_scalar_prefetch=1,
            grid=(blocks,),
            in_specs=in_specs,
            out_specs=out_specs,
            scratch_shapes=scratch,
        ),
        out_shape=out_shape,
        input_output_aliases=aliases,
        compiler_params=pltpu.CompilerParams(vmem_limit_bytes=24 * MIB),
        cost_estimate=pl.CostEstimate(
            flops=2 * rows * count * (dt + ds) * vocab,
            bytes_accessed=2 * count * (dt + ds) * vocab,
            transcendentals=2 * rows * vocab if last else 0,
        ),
        name="stage_last" if last else "stage",
    )(offs, *args)


def grad_kernel(block, off_ref, stats, tops, t_exp, s_exp, ws, kl, own, other, total, lse):
    step = pl.program_id(0)
    vocab, rows = t_exp.shape
    half = rows // 2

    @pl.when(step == 0)
    def _():
        me = off_ref[off_ref.shape[0] - 1]
        sides = []
        for chip in range(stats.shape[0] // 2):
            sides.append(stats[2 * chip + me])
            mate = stats[2 * chip + 1 - me]
            sides.append(jnp.concatenate([mate[:, half:], mate[:, :half]], axis=1))
        t_top = functools.reduce(jnp.maximum, [side[0:1] for side in sides])
        s_top = functools.reduce(jnp.maximum, [side[3:4] for side in sides])
        t_sum = sum(side[1:2] * jnp.exp(side[0:1] - t_top) for side in sides)
        cross = sum(side[2:3] * jnp.exp(side[0:1] - t_top) for side in sides)
        s_sum = sum(side[4:5] * jnp.exp(side[3:4] - s_top) for side in sides)
        t_lse = t_top + jnp.log(t_sum)
        s_lse = s_top + jnp.log(s_sum)
        lse[0:1, :] = t_lse
        lse[1:2, :] = s_lse
        kl[...] = cross / t_sum - t_lse + s_lse
        total[...] = jnp.zeros_like(total)

    def add(size):
        here = pl.ds(pl.multiple_of(step * block, 8), size)
        t_scale = jnp.exp(tops[step, 0:1, :] - lse[0:1, :])
        s_scale = jnp.exp(tops[step, 1:2, :] - lse[1:2, :])
        grad = (s_exp[here, :] * s_scale - t_exp[here, :] * t_scale).astype(bf16)
        total[...] += lax.dot_general(grad, ws[:size], TN, preferred_element_type=f32)

    by_block(step, vocab, block, add)

    @pl.when(step == pl.num_programs(0) - 1)
    def _():
        width = own.shape[2]
        for dest in range(own.shape[0]):
            own[dest] = total[:half, dest * width : (dest + 1) * width]
            other[dest] = total[half:, dest * width : (dest + 1) * width].astype(bf16)


def grad_partial(offs, stats, tops, t_exp, s_exp, ws, count):
    vocab, rows = t_exp.shape
    features = ws.shape[1]
    block = min(last_block, vocab)
    shares = (count, rows // 2, features // count)

    def still(array):
        return pl.BlockSpec(
            array.shape, lambda j, o: (0, 0, 0), pipeline_mode=pl.Buffered(1)
        )

    return pl.pallas_call(
        functools.partial(grad_kernel, block),
        grid_spec=pltpu.PrefetchScalarGridSpec(
            num_scalar_prefetch=1,
            grid=(pl.cdiv(vocab, block),),
            in_specs=[
                still(stats),
                still(tops),
                WHOLE,
                WHOLE,
                pl.BlockSpec((block, features), lambda j, o: (j, 0)),
            ],
            out_specs=[
                pl.BlockSpec((1, rows), lambda j, o: (0, 0)),
                pl.BlockSpec(shares, lambda j, o: (0, 0, 0)),
                pl.BlockSpec(shares, lambda j, o: (0, 0, 0)),
            ],
            scratch_shapes=[pltpu.VMEM((rows, features), f32), pltpu.VMEM((8, rows), f32)],
        ),
        out_shape=[
            jax.ShapeDtypeStruct((1, rows), f32),
            jax.ShapeDtypeStruct(shares, f32),
            jax.ShapeDtypeStruct(shares, bf16),
        ],
        compiler_params=pltpu.CompilerParams(vmem_limit_bytes=24 * MIB),
        cost_estimate=pl.CostEstimate(
            flops=2 * rows * features * vocab,
            bytes_accessed=2 * features * vocab,
            transcendentals=0,
        ),
        name="grad",
    )(offs, stats, tops, pinned(t_exp), pinned(s_exp), ws)


def ring_order(count):
    return list(range(0, count, 2)) + list(range(count - 1, 0, -2))


def ringed(teacher_hidden, teacher_weight, student_hidden, student_weight, loss_mask):
    count = lax.axis_size("vocab")
    dt, ds = teacher_hidden.shape[1], student_hidden.shape[1]
    order = ring_order(count)
    place = {device: at for at, device in enumerate(order)}
    table = [[order[(place[d] + k) % count] for k in range(count)] for d in range(count)]
    offs = lax.dynamic_index_in_dim(
        jnp.array(table, jnp.int32), lax.axis_index("vocab"), 0, False
    )
    offs = jnp.concatenate([offs, lax.axis_index("tok").astype(jnp.int32)[None]])
    up = [(order[i], order[(i + 1) % count]) for i in range(count)]
    down = [(b, a) for a, b in up]

    def sibling(array):
        return lax.ppermute(array, "tok", SWAP)

    mine = jnp.concatenate([teacher_hidden, student_hidden], axis=1)
    half = mine.shape[0] // 2
    wt, ws = teacher_weight.T, student_weight.T
    from_low = from_high = mine
    run = functools.partial(stage, offs=offs, wt=wt, ws=ws, dt=dt, ds=ds)
    held, waiting, picks = None, [(mine, sibling(mine))], (0,)
    for hop in range(1, count // 2 + 1):
        final = hop == count // 2
        next_low = lax.ppermute(from_low[:half] if final else from_low, "vocab", up)
        next_high = lax.ppermute(from_high[half:] if final else from_high, "vocab", down)
        held = run(waiting, picks, held=held)
        from_low, from_high, *held = lax.optimization_barrier((next_low, next_high, *held))
        if final:
            waiting = [(from_low, from_high, sibling(from_low), sibling(from_high))]
            picks = (hop,)
        else:
            waiting = [(from_low, sibling(from_low)), (from_high, sibling(from_high))]
            picks = (count - hop, hop)
    t_exp, s_exp, tops, stats = run(waiting, picks, held=held, copies=2 * count)
    every = lax.all_to_all(stats, ("vocab", "tok"), 0, 0, tiled=True)
    kl, own, other = grad_partial(offs, every, tops, t_exp, s_exp, ws, count)
    rows = teacher_hidden.shape[0]
    partial = (own + sibling(other).astype(f32)).astype(bf16)
    shares = lax.all_to_all(partial, "vocab", 0, 0, tiled=True)
    mask = loss_scale * loss_mask.astype(f32)
    grad = mask[:, None] * jnp.sum(shares.astype(f32), axis=0)
    return (kl[0, :rows], grad.astype(bf16))


def gathered(teacher_hidden, teacher_weight, student_hidden, student_weight, loss_mask):
    axes = ("vocab", "tok")

    def every_row(hidden):
        own = lax.all_gather(hidden, "vocab", axis=1, tiled=True)
        return lax.all_gather(own, "tok", axis=0, tiled=True)

    t = jnp.dot(every_row(teacher_hidden), teacher_weight, preferred_element_type=f32)
    s = jnp.dot(every_row(student_hidden), student_weight, preferred_element_type=f32)

    def log_total(logits):
        top = lax.pmax(jnp.max(logits, axis=1), axes)
        return top + jnp.log(lax.psum(jnp.sum(jnp.exp(logits - top[:, None]), axis=1), axes))

    t_log = t - log_total(t)[:, None]
    s_log = s - log_total(s)[:, None]
    teacher = jnp.exp(t_log)
    kl = lax.psum(jnp.sum(teacher * (t_log - s_log), axis=1), axes)
    grad = (jnp.exp(s_log) - teacher).astype(bf16)
    part = lax.dot_general(grad, student_weight, NT, preferred_element_type=f32)
    part = lax.psum_scatter(part, "tok", scatter_dimension=0, tiled=True)
    part = lax.psum_scatter(part, "vocab", scatter_dimension=1, tiled=True)
    rows = teacher_hidden.shape[0]
    mask = loss_scale * loss_mask.astype(f32)
    kl = lax.dynamic_slice_in_dim(kl, lax.axis_index("tok") * rows, rows)
    return (kl, (mask[:, None] * part).astype(bf16))


def shards(teacher_hidden, teacher_weight, student_hidden, student_weight, loss_mask):
    count = lax.axis_size("vocab")
    lanes = teacher_hidden.shape[1] % 128 == 0 and student_hidden.shape[1] % 128 == 0
    rows = teacher_hidden.shape[0] % 32 == 0 and teacher_weight.shape[1] % 16 == 0
    fits = lanes and rows and count % 2 == 0 and count >= 4 and lax.axis_size("tok") == 2
    run = ringed if fits else gathered
    return run(teacher_hidden, teacher_weight, student_hidden, student_weight, loss_mask)


def solution(mesh):
    return jax.shard_map(
        shards,
        mesh=mesh,
        in_specs=(
            P(("groups", "tok"), "vocab"),
            P(None, ("vocab", "tok")),
            P(("groups", "tok"), "vocab"),
            P(None, ("vocab", "tok")),
            P(("groups", "tok")),
        ),
        out_specs=(P(("groups", "tok")), P(("groups", "tok"), "vocab")),
        check_vma=False,
    )
```

```python
import functools

import jax
import jax.numpy as jnp
from jax import lax
from jax.experimental import pallas as pl
from jax.experimental.pallas import tpu as pltpu
from jax.sharding import PartitionSpec as P

loss_scale = 16.0
f32 = jnp.float32
bf16 = jnp.bfloat16
MIB = 1 << 20
last_block = 1024
NT = (((1,), (1,)), ((), ()))
TN = (((0,), (0,)), ((), ()))
WHOLE = pl.BlockSpec(memory_space=pltpu.VMEM)
SWAP = ((0, 1), (1, 0))


def rows_per_block(rows, cap):
    for count in range(1, rows // 8 + 1):
        if rows % (8 * count) == 0 and rows // count <= cap:
            return rows // count
    return rows


def pinned(array):
    return pltpu.with_memory_space_constraint(array, pltpu.VMEM)


def stage_kernel(count, pieces, dt, first, block, off_ref, *refs):
    refs = list(refs)

    def take(number):
        taken = refs[:number]
        del refs[:number]
        return taken

    parts = take(count * pieces)
    wt, ws = take(count), take(count)
    held = None if first else take(2)
    t_out, s_out = take(2)
    tops, stats = take(2) if len(refs) > 2 else (None, None)
    xt, xs, run = take(3) if tops is not None else (None, None, None)
    step, steps = pl.program_id(0), pl.num_programs(0)
    vocab, rows = t_out.shape

    if run is not None:

        @pl.when(step == 0)
        def _():
            for shard in range(count):
                at = 0
                for part in parts[shard * pieces : (shard + 1) * pieces]:
                    span = pl.ds(at, part.shape[0])
                    xt[shard, span, :] = part[:, :dt]
                    xs[shard, span, :] = part[:, dt:]
                    at += part.shape[0]
            run[...] = jnp.zeros_like(run)
            run[0:1, :] = jnp.full((1, rows), -jnp.inf, f32)
            run[3:4, :] = jnp.full((1, rows), -jnp.inf, f32)

    def multiply(size):
        here = pl.ds(pl.multiple_of(step * block, 8), size)
        if run is None:
            at = 0
            for piece in range(pieces):
                width = parts[piece].shape[0]
                cols = pl.ds(at, width)
                at += width
                for out, prior, weight, low, high in (
                    (t_out, 0, wt, 0, dt),
                    (s_out, 1, ws, dt, parts[piece].shape[1]),
                ):
                    value = None if first else held[prior][here, cols]
                    for shard in range(count):
                        add = lax.dot_general(
                            weight[shard][:size],
                            parts[shard * pieces + piece][:, low:high],
                            NT,
                            preferred_element_type=f32,
                        )
                        value = add if value is None else value + add
                    out[here, cols] = value
            return
        t = s = None
        for shard in range(count):
            t_add = lax.dot_general(wt[shard][:size], xt[shard], NT, preferred_element_type=f32)
            s_add = lax.dot_general(ws[shard][:size], xs[shard], NT, preferred_element_type=f32)
            t = t_add if t is None else t + t_add
            s = s_add if s is None else s + s_add
        t = t + held[0][here, :]
        s = s + held[1][here, :]
        t_top = jnp.max(t, axis=0, keepdims=True)
        s_top = jnp.max(s, axis=0, keepdims=True)
        t_exp = jnp.exp(t - t_top)
        s_exp = jnp.exp(s - s_top)
        t_out[here, :] = t_exp
        s_out[here, :] = s_exp
        tops[step, 0:1, :] = t_top
        tops[step, 1:2, :] = s_top
        t_new = jnp.maximum(run[0:1, :], t_top)
        s_new = jnp.maximum(run[3:4, :], s_top)
        t_old, t_add = jnp.exp(run[0:1, :] - t_new), jnp.exp(t_top - t_new)
        s_old, s_add = jnp.exp(run[3:4, :] - s_new), jnp.exp(s_top - s_new)
        t_sum = jnp.sum(t_exp, axis=0, keepdims=True)
        cross = jnp.sum(t_exp * (t - s), axis=0, keepdims=True)
        s_sum = jnp.sum(s_exp, axis=0, keepdims=True)
        run[1:2, :] = run[1:2, :] * t_old + t_sum * t_add
        run[2:3, :] = run[2:3, :] * t_old + cross * t_add
        run[4:5, :] = run[4:5, :] * s_old + s_sum * s_add
        run[0:1, :] = t_new
        run[3:4, :] = s_new

    by_block(step, vocab, block, multiply)
    if run is not None:

        @pl.when(step == steps - 1)
        def _():
            for dest in range(stats.shape[0]):
                stats[dest] = run[...]


def by_block(step, vocab, block, body):
    whole, tail = vocab // block, vocab % block
    if tail == 0:
        body(block)
        return
    if whole > 0:
        pl.when(step < whole)(functools.partial(body, block))
    pl.when(step == whole)(functools.partial(body, tail))


def stage(shards, picks, offs, wt, ws, held, dt, ds, copies=0):
    count, pieces = len(shards), len(shards[0])
    vocab = wt.shape[0]
    last = copies > 0
    rows = sum(part.shape[0] for part in shards[0])
    block = last_block if last else rows_per_block(vocab, 800)
    block = min(block, vocab)
    blocks = pl.cdiv(vocab, block)
    parts = [part for shard in shards for part in shard]
    in_specs = [WHOLE] * len(parts)
    for width in (dt, ds):
        in_specs += [
            pl.BlockSpec((block, width), lambda j, o, pick=pick: (j, o[pick])) for pick in picks
        ]
    args = [pinned(part) for part in parts] + [wt] * count + [ws] * count
    aliases = {}
    if held is not None:
        aliases = {1 + len(args): 0, 2 + len(args): 1}
        in_specs += [WHOLE, WHOLE]
        args += [pinned(array) for array in held]
    out_shape, out_specs = [pltpu.VMEM((vocab, rows), f32)] * 2, [WHOLE, WHOLE]
    scratch = []
    if last:
        for shape in ((blocks, 8, rows), (copies, 8, rows)):
            out_shape.append(jax.ShapeDtypeStruct(shape, f32))
            out_specs.append(pl.BlockSpec(shape, lambda j, o: (0, 0, 0)))
        scratch += [pltpu.VMEM((count, rows, width), bf16) for width in (dt, ds)]
        scratch.append(pltpu.VMEM((8, rows), f32))
    return pl.pallas_call(
        functools.partial(stage_kernel, count, pieces, dt, held is None, block),
        grid_spec=pltpu.PrefetchScalarGridSpec(
            num_scalar_prefetch=1,
            grid=(blocks,),
            in_specs=in_specs,
            out_specs=out_specs,
            scratch_shapes=scratch,
        ),
        out_shape=out_shape,
        input_output_aliases=aliases,
        compiler_params=pltpu.CompilerParams(vmem_limit_bytes=24 * MIB),
        cost_estimate=pl.CostEstimate(
            flops=2 * rows * count * (dt + ds) * vocab,
            bytes_accessed=2 * count * (dt + ds) * vocab,
            transcendentals=2 * rows * vocab if last else 0,
        ),
        name="stage_last" if last else "stage",
    )(offs, *args)


def grad_kernel(block, off_ref, stats, tops, t_exp, s_exp, ws, kl, own, other, total, lse):
    step = pl.program_id(0)
    vocab, rows = t_exp.shape
    half = rows // 2

    @pl.when(step == 0)
    def _():
        me = off_ref[off_ref.shape[0] - 1]
        sides = []
        for chip in range(stats.shape[0] // 2):
            sides.append(stats[2 * chip + me])
            mate = stats[2 * chip + 1 - me]
            sides.append(jnp.concatenate([mate[:, half:], mate[:, :half]], axis=1))
        t_top = functools.reduce(jnp.maximum, [side[0:1] for side in sides])
        s_top = functools.reduce(jnp.maximum, [side[3:4] for side in sides])
        t_sum = sum(side[1:2] * jnp.exp(side[0:1] - t_top) for side in sides)
        cross = sum(side[2:3] * jnp.exp(side[0:1] - t_top) for side in sides)
        s_sum = sum(side[4:5] * jnp.exp(side[3:4] - s_top) for side in sides)
        t_lse = t_top + jnp.log(t_sum)
        s_lse = s_top + jnp.log(s_sum)
        lse[0:1, :] = t_lse
        lse[1:2, :] = s_lse
        kl[...] = cross / t_sum - t_lse + s_lse
        total[...] = jnp.zeros_like(total)

    def add(size):
        here = pl.ds(pl.multiple_of(step * block, 8), size)
        t_scale = jnp.exp(tops[step, 0:1, :] - lse[0:1, :])
        s_scale = jnp.exp(tops[step, 1:2, :] - lse[1:2, :])
        grad = (s_exp[here, :] * s_scale - t_exp[here, :] * t_scale).astype(bf16)
        total[...] += lax.dot_general(grad, ws[:size], TN, preferred_element_type=f32)

    by_block(step, vocab, block, add)

    @pl.when(step == pl.num_programs(0) - 1)
    def _():
        width = own.shape[2]
        for dest in range(own.shape[0]):
            own[dest] = total[:half, dest * width : (dest + 1) * width]
            other[dest] = total[half:, dest * width : (dest + 1) * width].astype(bf16)


def grad_partial(offs, stats, tops, t_exp, s_exp, ws, count):
    vocab, rows = t_exp.shape
    features = ws.shape[1]
    block = min(last_block, vocab)
    shares = (count, rows // 2, features // count)

    def still(array):
        return pl.BlockSpec(
            array.shape, lambda j, o: (0, 0, 0), pipeline_mode=pl.Buffered(1)
        )

    return pl.pallas_call(
        functools.partial(grad_kernel, block),
        grid_spec=pltpu.PrefetchScalarGridSpec(
            num_scalar_prefetch=1,
            grid=(pl.cdiv(vocab, block),),
            in_specs=[
                still(stats),
                still(tops),
                WHOLE,
                WHOLE,
                pl.BlockSpec((block, features), lambda j, o: (j, 0)),
            ],
            out_specs=[
                pl.BlockSpec((1, rows), lambda j, o: (0, 0)),
                pl.BlockSpec(shares, lambda j, o: (0, 0, 0)),
                pl.BlockSpec(shares, lambda j, o: (0, 0, 0)),
            ],
            scratch_shapes=[pltpu.VMEM((rows, features), f32), pltpu.VMEM((8, rows), f32)],
        ),
        out_shape=[
            jax.ShapeDtypeStruct((1, rows), f32),
            jax.ShapeDtypeStruct(shares, f32),
            jax.ShapeDtypeStruct(shares, bf16),
        ],
        compiler_params=pltpu.CompilerParams(vmem_limit_bytes=24 * MIB),
        cost_estimate=pl.CostEstimate(
            flops=2 * rows * features * vocab,
            bytes_accessed=2 * features * vocab,
            transcendentals=0,
        ),
        name="grad",
    )(offs, stats, tops, pinned(t_exp), pinned(s_exp), ws)


def ring_order(count):
    return list(range(0, count, 2)) + list(range(count - 1, 0, -2))


def ringed(teacher_hidden, teacher_weight, student_hidden, student_weight, loss_mask):
    count = lax.axis_size("vocab")
    dt, ds = teacher_hidden.shape[1], student_hidden.shape[1]
    order = ring_order(count)
    place = {device: at for at, device in enumerate(order)}
    table = [[order[(place[d] + k) % count] for k in range(count)] for d in range(count)]
    offs = lax.dynamic_index_in_dim(
        jnp.array(table, jnp.int32), lax.axis_index("vocab"), 0, False
    )
    offs = jnp.concatenate([offs, lax.axis_index("tok").astype(jnp.int32)[None]])
    up = [(order[i], order[(i + 1) % count]) for i in range(count)]
    down = [(b, a) for a, b in up]

    def sibling(array):
        return lax.ppermute(array, "tok", SWAP)

    mine = jnp.concatenate([teacher_hidden, student_hidden], axis=1)
    half = mine.shape[0] // 2
    wt, ws = teacher_weight.T, student_weight.T
    from_low = from_high = mine
    run = functools.partial(stage, offs=offs, wt=wt, ws=ws, dt=dt, ds=ds)
    held, waiting, picks = None, [(mine, sibling(mine))], (0,)
    for hop in range(1, count // 2 + 1):
        final = hop == count // 2
        next_low = lax.ppermute(from_low[:half] if final else from_low, "vocab", up)
        next_high = lax.ppermute(from_high[half:] if final else from_high, "vocab", down)
        held = run(waiting, picks, held=held)
        from_low, from_high, *held = lax.optimization_barrier((next_low, next_high, *held))
        if final:
            waiting = [(from_low, from_high, sibling(from_low), sibling(from_high))]
            picks = (hop,)
        else:
            waiting = [(from_low, sibling(from_low)), (from_high, sibling(from_high))]
            picks = (count - hop, hop)
    t_exp, s_exp, tops, stats = run(waiting, picks, held=held, copies=2 * count)
    every = lax.all_to_all(stats, ("vocab", "tok"), 0, 0, tiled=True)
    kl, own, other = grad_partial(offs, every, tops, t_exp, s_exp, ws, count)
    rows = teacher_hidden.shape[0]
    partial = (own + sibling(other).astype(f32)).astype(bf16)
    here = lax.axis_index("vocab")
    total = lax.dynamic_index_in_dim(partial, here, 0, False).astype(f32)
    wing = count // 2
    for shift in list(range(wing, count)) + list(range(1, wing)):
        pairs = [(chip, (chip + shift) % count) for chip in range(count)]
        share = lax.dynamic_index_in_dim(partial, (here + shift) % count, 0, False)
        total = total + lax.ppermute(share, "vocab", pairs).astype(f32)
    mask = loss_scale * loss_mask.astype(f32)
    return (kl[0, :rows], (mask[:, None] * total).astype(bf16))


def gathered(teacher_hidden, teacher_weight, student_hidden, student_weight, loss_mask):
    axes = ("vocab", "tok")

    def every_row(hidden):
        own = lax.all_gather(hidden, "vocab", axis=1, tiled=True)
        return lax.all_gather(own, "tok", axis=0, tiled=True)

    t = jnp.dot(every_row(teacher_hidden), teacher_weight, preferred_element_type=f32)
    s = jnp.dot(every_row(student_hidden), student_weight, preferred_element_type=f32)

    def log_total(logits):
        top = lax.pmax(jnp.max(logits, axis=1), axes)
        return top + jnp.log(lax.psum(jnp.sum(jnp.exp(logits - top[:, None]), axis=1), axes))

    t_log = t - log_total(t)[:, None]
    s_log = s - log_total(s)[:, None]
    teacher = jnp.exp(t_log)
    kl = lax.psum(jnp.sum(teacher * (t_log - s_log), axis=1), axes)
    grad = (jnp.exp(s_log) - teacher).astype(bf16)
    part = lax.dot_general(grad, student_weight, NT, preferred_element_type=f32)
    part = lax.psum_scatter(part, "tok", scatter_dimension=0, tiled=True)
    part = lax.psum_scatter(part, "vocab", scatter_dimension=1, tiled=True)
    rows = teacher_hidden.shape[0]
    mask = loss_scale * loss_mask.astype(f32)
    kl = lax.dynamic_slice_in_dim(kl, lax.axis_index("tok") * rows, rows)
    return (kl, (mask[:, None] * part).astype(bf16))


def shards(teacher_hidden, teacher_weight, student_hidden, student_weight, loss_mask):
    count = lax.axis_size("vocab")
    lanes = teacher_hidden.shape[1] % 128 == 0 and student_hidden.shape[1] % 128 == 0
    rows = teacher_hidden.shape[0] % 32 == 0 and teacher_weight.shape[1] % 16 == 0
    fits = lanes and rows and count % 2 == 0 and count >= 4 and lax.axis_size("tok") == 2
    run = ringed if fits else gathered
    return run(teacher_hidden, teacher_weight, student_hidden, student_weight, loss_mask)


def solution(mesh):
    return jax.shard_map(
        shards,
        mesh=mesh,
        in_specs=(
            P(("groups", "tok"), "vocab"),
            P(None, ("vocab", "tok")),
            P(("groups", "tok"), "vocab"),
            P(None, ("vocab", "tok")),
            P(("groups", "tok")),
        ),
        out_specs=(P(("groups", "tok")), P(("groups", "tok"), "vocab")),
        check_vma=False,
    )
```

```python
import functools

import jax
import jax.numpy as jnp
from jax import lax
from jax.experimental import pallas as pl
from jax.experimental.pallas import tpu as pltpu
from jax.sharding import PartitionSpec as P

loss_scale = 16.0
f32 = jnp.float32
bf16 = jnp.bfloat16
MIB = 1 << 20
last_block = 1024
NT = (((1,), (1,)), ((), ()))
TN = (((0,), (0,)), ((), ()))
WHOLE = pl.BlockSpec(memory_space=pltpu.VMEM)
SWAP = ((0, 1), (1, 0))


def rows_per_block(rows, cap):
    for count in range(1, rows // 8 + 1):
        if rows % (8 * count) == 0 and rows // count <= cap:
            return rows // count
    return rows


def pinned(array):
    return pltpu.with_memory_space_constraint(array, pltpu.VMEM)


def stage_kernel(count, pieces, dt, first, block, off_ref, *refs):
    refs = list(refs)

    def take(number):
        taken = refs[:number]
        del refs[:number]
        return taken

    parts = take(count * pieces)
    wt, ws = take(count), take(count)
    held = None if first else take(2)
    t_out, s_out = take(2)
    tops, stats = take(2) if len(refs) > 2 else (None, None)
    xt, xs, run = take(3) if tops is not None else (None, None, None)
    step, steps = pl.program_id(0), pl.num_programs(0)
    vocab, rows = t_out.shape

    if run is not None:

        @pl.when(step == 0)
        def _():
            for shard in range(count):
                at = 0
                for part in parts[shard * pieces : (shard + 1) * pieces]:
                    span = pl.ds(at, part.shape[0])
                    xt[shard, span, :] = part[:, :dt]
                    xs[shard, span, :] = part[:, dt:]
                    at += part.shape[0]
            run[...] = jnp.zeros_like(run)
            run[0:1, :] = jnp.full((1, rows), -jnp.inf, f32)
            run[3:4, :] = jnp.full((1, rows), -jnp.inf, f32)

    def multiply(size):
        here = pl.ds(pl.multiple_of(step * block, 8), size)
        if run is None:
            at = 0
            for piece in range(pieces):
                width = parts[piece].shape[0]
                cols = pl.ds(at, width)
                at += width
                for out, prior, weight, low, high in (
                    (t_out, 0, wt, 0, dt),
                    (s_out, 1, ws, dt, parts[piece].shape[1]),
                ):
                    value = None if first else held[prior][here, cols]
                    for shard in range(count):
                        add = lax.dot_general(
                            weight[shard][:size],
                            parts[shard * pieces + piece][:, low:high],
                            NT,
                            preferred_element_type=f32,
                        )
                        value = add if value is None else value + add
                    out[here, cols] = value
            return
        t = s = None
        for shard in range(count):
            t_add = lax.dot_general(wt[shard][:size], xt[shard], NT, preferred_element_type=f32)
            s_add = lax.dot_general(ws[shard][:size], xs[shard], NT, preferred_element_type=f32)
            t = t_add if t is None else t + t_add
            s = s_add if s is None else s + s_add
        t = t + held[0][here, :]
        s = s + held[1][here, :]
        t_top = jnp.max(t, axis=0, keepdims=True)
        s_top = jnp.max(s, axis=0, keepdims=True)
        t_exp = jnp.exp(t - t_top)
        s_exp = jnp.exp(s - s_top)
        t_out[here, :] = t_exp
        s_out[here, :] = s_exp
        tops[step, 0:1, :] = t_top
        tops[step, 1:2, :] = s_top
        t_new = jnp.maximum(run[0:1, :], t_top)
        s_new = jnp.maximum(run[3:4, :], s_top)
        t_old, t_add = jnp.exp(run[0:1, :] - t_new), jnp.exp(t_top - t_new)
        s_old, s_add = jnp.exp(run[3:4, :] - s_new), jnp.exp(s_top - s_new)
        t_sum = jnp.sum(t_exp, axis=0, keepdims=True)
        cross = jnp.sum(t_exp * (t - s), axis=0, keepdims=True)
        s_sum = jnp.sum(s_exp, axis=0, keepdims=True)
        run[1:2, :] = run[1:2, :] * t_old + t_sum * t_add
        run[2:3, :] = run[2:3, :] * t_old + cross * t_add
        run[4:5, :] = run[4:5, :] * s_old + s_sum * s_add
        run[0:1, :] = t_new
        run[3:4, :] = s_new

    by_block(step, vocab, block, multiply)
    if run is not None:

        @pl.when(step == steps - 1)
        def _():
            for dest in range(stats.shape[0]):
                stats[dest] = run[...]


def by_block(step, vocab, block, body):
    whole, tail = vocab // block, vocab % block
    if tail == 0:
        body(block)
        return
    if whole > 0:
        pl.when(step < whole)(functools.partial(body, block))
    pl.when(step == whole)(functools.partial(body, tail))


def stage(shards, picks, offs, wt, ws, held, dt, ds, copies=0):
    count, pieces = len(shards), len(shards[0])
    vocab = wt.shape[0]
    last = copies > 0
    rows = sum(part.shape[0] for part in shards[0])
    block = last_block if last else rows_per_block(vocab, 800)
    block = min(block, vocab)
    blocks = pl.cdiv(vocab, block)
    parts = [part for shard in shards for part in shard]
    in_specs = [WHOLE] * len(parts)
    for width in (dt, ds):
        in_specs += [
            pl.BlockSpec((block, width), lambda j, o, pick=pick: (j, o[pick])) for pick in picks
        ]
    args = [pinned(part) for part in parts] + [wt] * count + [ws] * count
    aliases = {}
    if held is not None:
        aliases = {1 + len(args): 0, 2 + len(args): 1}
        in_specs += [WHOLE, WHOLE]
        args += [pinned(array) for array in held]
    out_shape, out_specs = [pltpu.VMEM((vocab, rows), f32)] * 2, [WHOLE, WHOLE]
    scratch = []
    if last:
        for shape in ((blocks, 8, rows), (copies, 8, rows)):
            out_shape.append(jax.ShapeDtypeStruct(shape, f32))
            out_specs.append(WHOLE)
        scratch += [pltpu.VMEM((count, rows, width), bf16) for width in (dt, ds)]
        scratch.append(pltpu.VMEM((8, rows), f32))
    return pl.pallas_call(
        functools.partial(stage_kernel, count, pieces, dt, held is None, block),
        grid_spec=pltpu.PrefetchScalarGridSpec(
            num_scalar_prefetch=1,
            grid=(blocks,),
            in_specs=in_specs,
            out_specs=out_specs,
            scratch_shapes=scratch,
        ),
        out_shape=out_shape,
        input_output_aliases=aliases,
        compiler_params=pltpu.CompilerParams(vmem_limit_bytes=24 * MIB),
        cost_estimate=pl.CostEstimate(
            flops=2 * rows * count * (dt + ds) * vocab,
            bytes_accessed=2 * count * (dt + ds) * vocab,
            transcendentals=2 * rows * vocab if last else 0,
        ),
        name="stage_last" if last else "stage",
    )(offs, *args)


def grad_kernel(block, off_ref, stats, tops, t_exp, s_exp, ws, kl, own, other, total, lse):
    step = pl.program_id(0)
    vocab, rows = t_exp.shape
    half = rows // 2

    @pl.when(step == 0)
    def _():
        me = off_ref[off_ref.shape[0] - 1]
        sides = []
        for chip in range(stats.shape[0] // 2):
            sides.append(stats[2 * chip + me])
            mate = stats[2 * chip + 1 - me]
            sides.append(jnp.concatenate([mate[:, half:], mate[:, :half]], axis=1))
        t_top = functools.reduce(jnp.maximum, [side[0:1] for side in sides])
        s_top = functools.reduce(jnp.maximum, [side[3:4] for side in sides])
        t_sum = sum(side[1:2] * jnp.exp(side[0:1] - t_top) for side in sides)
        cross = sum(side[2:3] * jnp.exp(side[0:1] - t_top) for side in sides)
        s_sum = sum(side[4:5] * jnp.exp(side[3:4] - s_top) for side in sides)
        t_lse = t_top + jnp.log(t_sum)
        s_lse = s_top + jnp.log(s_sum)
        lse[0:1, :] = t_lse
        lse[1:2, :] = s_lse
        kl[...] = cross / t_sum - t_lse + s_lse
        total[...] = jnp.zeros_like(total)

    def add(size):
        here = pl.ds(pl.multiple_of(step * block, 8), size)
        t_scale = jnp.exp(tops[step, 0:1, :] - lse[0:1, :])
        s_scale = jnp.exp(tops[step, 1:2, :] - lse[1:2, :])
        grad = (s_exp[here, :] * s_scale - t_exp[here, :] * t_scale).astype(bf16)
        total[...] += lax.dot_general(grad, ws[:size], TN, preferred_element_type=f32)

    by_block(step, vocab, block, add)

    @pl.when(step == pl.num_programs(0) - 1)
    def _():
        width = own.shape[2]
        for dest in range(own.shape[0]):
            own[dest] = total[:half, dest * width : (dest + 1) * width]
            other[dest] = total[half:, dest * width : (dest + 1) * width].astype(bf16)


def grad_partial(offs, stats, tops, t_exp, s_exp, ws, count):
    vocab, rows = t_exp.shape
    features = ws.shape[1]
    block = min(last_block, vocab)
    shares = (count, rows // 2, features // count)

    return pl.pallas_call(
        functools.partial(grad_kernel, block),
        grid_spec=pltpu.PrefetchScalarGridSpec(
            num_scalar_prefetch=1,
            grid=(pl.cdiv(vocab, block),),
            in_specs=[
                WHOLE,
                WHOLE,
                WHOLE,
                WHOLE,
                pl.BlockSpec((block, features), lambda j, o: (j, 0)),
            ],
            out_specs=[WHOLE, WHOLE, WHOLE],
            scratch_shapes=[pltpu.VMEM((rows, features), f32), pltpu.VMEM((8, rows), f32)],
        ),
        out_shape=[
            jax.ShapeDtypeStruct((1, rows), f32),
            jax.ShapeDtypeStruct(shares, f32),
            jax.ShapeDtypeStruct(shares, bf16),
        ],
        compiler_params=pltpu.CompilerParams(vmem_limit_bytes=24 * MIB),
        cost_estimate=pl.CostEstimate(
            flops=2 * rows * features * vocab,
            bytes_accessed=2 * features * vocab,
            transcendentals=0,
        ),
        name="grad",
    )(offs, stats, tops, pinned(t_exp), pinned(s_exp), ws)


def ring_order(count):
    return list(range(0, count, 2)) + list(range(count - 1, 0, -2))


def ringed(teacher_hidden, teacher_weight, student_hidden, student_weight, loss_mask):
    count = lax.axis_size("vocab")
    dt, ds = teacher_hidden.shape[1], student_hidden.shape[1]
    order = ring_order(count)
    place = {device: at for at, device in enumerate(order)}
    table = [[order[(place[d] + k) % count] for k in range(count)] for d in range(count)]
    offs = lax.dynamic_index_in_dim(
        jnp.array(table, jnp.int32), lax.axis_index("vocab"), 0, False
    )
    offs = jnp.concatenate([offs, lax.axis_index("tok").astype(jnp.int32)[None]])
    up = [(order[i], order[(i + 1) % count]) for i in range(count)]
    down = [(b, a) for a, b in up]

    def sibling(array):
        return lax.ppermute(array, "tok", SWAP)

    mine = jnp.concatenate([teacher_hidden, student_hidden], axis=1)
    half = mine.shape[0] // 2
    wt, ws = teacher_weight.T, student_weight.T
    from_low = from_high = mine
    run = functools.partial(stage, offs=offs, wt=wt, ws=ws, dt=dt, ds=ds)
    held, waiting, picks = None, [(mine, sibling(mine))], (0,)
    for hop in range(1, count // 2 + 1):
        final = hop == count // 2
        next_low = lax.ppermute(from_low[:half] if final else from_low, "vocab", up)
        next_high = lax.ppermute(from_high[half:] if final else from_high, "vocab", down)
        held = run(waiting, picks, held=held)
        from_low, from_high, *held = lax.optimization_barrier((next_low, next_high, *held))
        if final:
            waiting = [(from_low, from_high, sibling(from_low), sibling(from_high))]
            picks = (hop,)
        else:
            waiting = [(from_low, sibling(from_low)), (from_high, sibling(from_high))]
            picks = (count - hop, hop)
    t_exp, s_exp, tops, stats = run(waiting, picks, held=held, copies=2 * count)
    every = lax.all_to_all(stats, ("vocab", "tok"), 0, 0, tiled=True)
    kl, own, other = grad_partial(offs, every, tops, t_exp, s_exp, ws, count)
    rows = teacher_hidden.shape[0]
    beside = sibling(other)
    partial = (own + beside.astype(f32)).astype(bf16)
    chip, units = lax.axis_index("vocab"), count // 2
    middle = units // 2

    def goal(c, shift, flip):
        return (c // 2 + shift) % units * 2 + (c % 2 + flip) % 2

    def share(shift, flip):
        return lax.dynamic_index_in_dim(partial, goal(chip, shift, flip), 0, False)

    def exact(shift, flip):
        at = goal(chip, shift, flip)
        pair = [lax.dynamic_index_in_dim(array, at, 0, False) for array in (own, beside)]
        return pair[0] + pair[1].astype(f32)

    def sent(value, shift, flip):
        return lax.ppermute(value, "vocab", [(c, goal(c, shift, flip)) for c in range(count)])

    near = sent(jnp.stack([share(0, 1), share(middle, 1)]), 0, 1).astype(f32)
    total = exact(0, 0) + near[0]
    for shift in range(1, units):
        if shift != middle:
            for flip in range(2):
                total = total + sent(share(shift, flip), shift, flip).astype(f32)
    merged = (exact(middle, 0) + near[1]).astype(bf16)
    total = total + sent(merged, middle, 0).astype(f32)
    mask = loss_scale * loss_mask.astype(f32)
    return (kl[0, :rows], (mask[:, None] * total).astype(bf16))


def gathered(teacher_hidden, teacher_weight, student_hidden, student_weight, loss_mask):
    axes = ("vocab", "tok")

    def every_row(hidden):
        own = lax.all_gather(hidden, "vocab", axis=1, tiled=True)
        return lax.all_gather(own, "tok", axis=0, tiled=True)

    t = jnp.dot(every_row(teacher_hidden), teacher_weight, preferred_element_type=f32)
    s = jnp.dot(every_row(student_hidden), student_weight, preferred_element_type=f32)

    def log_total(logits):
        top = lax.pmax(jnp.max(logits, axis=1), axes)
        return top + jnp.log(lax.psum(jnp.sum(jnp.exp(logits - top[:, None]), axis=1), axes))

    t_log = t - log_total(t)[:, None]
    s_log = s - log_total(s)[:, None]
    teacher = jnp.exp(t_log)
    kl = lax.psum(jnp.sum(teacher * (t_log - s_log), axis=1), axes)
    grad = (jnp.exp(s_log) - teacher).astype(bf16)
    part = lax.dot_general(grad, student_weight, NT, preferred_element_type=f32)
    part = lax.psum_scatter(part, "tok", scatter_dimension=0, tiled=True)
    part = lax.psum_scatter(part, "vocab", scatter_dimension=1, tiled=True)
    rows = teacher_hidden.shape[0]
    mask = loss_scale * loss_mask.astype(f32)
    kl = lax.dynamic_slice_in_dim(kl, lax.axis_index("tok") * rows, rows)
    return (kl, (mask[:, None] * part).astype(bf16))


def shards(teacher_hidden, teacher_weight, student_hidden, student_weight, loss_mask):
    count = lax.axis_size("vocab")
    lanes = teacher_hidden.shape[1] % 128 == 0 and student_hidden.shape[1] % 128 == 0
    rows = teacher_hidden.shape[0] % 32 == 0 and teacher_weight.shape[1] % 16 == 0
    fits = lanes and rows and count % 2 == 0 and count >= 4 and lax.axis_size("tok") == 2
    run = ringed if fits else gathered
    return run(teacher_hidden, teacher_weight, student_hidden, student_weight, loss_mask)


def solution(mesh):
    return jax.shard_map(
        shards,
        mesh=mesh,
        in_specs=(
            P(("groups", "tok"), "vocab"),
            P(None, ("vocab", "tok")),
            P(("groups", "tok"), "vocab"),
            P(None, ("vocab", "tok")),
            P(("groups", "tok")),
        ),
        out_specs=(P(("groups", "tok")), P(("groups", "tok"), "vocab")),
        check_vma=False,
    )
```

```python
import functools

import jax
import jax.numpy as jnp
from jax import lax
from jax.experimental import pallas as pl
from jax.experimental.pallas import tpu as pltpu
from jax.sharding import PartitionSpec as P

loss_scale = 16.0
f32 = jnp.float32
bf16 = jnp.bfloat16
MIB = 1 << 20
last_block = 1024
NT = (((1,), (1,)), ((), ()))
TN = (((0,), (0,)), ((), ()))
WHOLE = pl.BlockSpec(memory_space=pltpu.VMEM)
SWAP = ((0, 1), (1, 0))


def rows_per_block(rows, cap):
    for count in range(1, rows // 8 + 1):
        if rows % (8 * count) == 0 and rows // count <= cap:
            return rows // count
    return rows


def pinned(array):
    return pltpu.with_memory_space_constraint(array, pltpu.VMEM)


def stage_kernel(count, pieces, dt, first, block, off_ref, *refs):
    refs = list(refs)

    def take(number):
        taken = refs[:number]
        del refs[:number]
        return taken

    parts = take(count * pieces)
    wt, ws = take(count), take(count)
    held = None if first else take(2)
    t_out, s_out = take(2)
    tops, stats = take(2) if len(refs) > 2 else (None, None)
    xt, xs, run = take(3) if tops is not None else (None, None, None)
    step, steps = pl.program_id(0), pl.num_programs(0)
    vocab, rows = t_out.shape

    if run is not None:

        @pl.when(step == 0)
        def _():
            for shard in range(count):
                at = 0
                for part in parts[shard * pieces : (shard + 1) * pieces]:
                    span = pl.ds(at, part.shape[0])
                    xt[shard, span, :] = part[:, :dt]
                    xs[shard, span, :] = part[:, dt:]
                    at += part.shape[0]
            run[...] = jnp.zeros_like(run)
            run[0:1, :] = jnp.full((1, rows), -jnp.inf, f32)
            run[3:4, :] = jnp.full((1, rows), -jnp.inf, f32)

    def multiply(size):
        here = pl.ds(pl.multiple_of(step * block, 8), size)
        if run is None:
            at = 0
            for piece in range(pieces):
                width = parts[piece].shape[0]
                cols = pl.ds(at, width)
                at += width
                for out, prior, weight, low, high in (
                    (t_out, 0, wt, 0, dt),
                    (s_out, 1, ws, dt, parts[piece].shape[1]),
                ):
                    value = None if first else held[prior][here, cols]
                    for shard in range(count):
                        add = lax.dot_general(
                            weight[shard][:size],
                            parts[shard * pieces + piece][:, low:high],
                            NT,
                            preferred_element_type=f32,
                        )
                        value = add if value is None else value + add
                    out[here, cols] = value
            return
        t = s = None
        for shard in range(count):
            t_add = lax.dot_general(wt[shard][:size], xt[shard], NT, preferred_element_type=f32)
            s_add = lax.dot_general(ws[shard][:size], xs[shard], NT, preferred_element_type=f32)
            t = t_add if t is None else t + t_add
            s = s_add if s is None else s + s_add
        t = t + held[0][here, :]
        s = s + held[1][here, :]
        t_top = jnp.max(t, axis=0, keepdims=True)
        s_top = jnp.max(s, axis=0, keepdims=True)
        t_exp = jnp.exp(t - t_top)
        s_exp = jnp.exp(s - s_top)
        t_out[here, :] = t_exp
        s_out[here, :] = s_exp
        tops[step, 0:1, :] = t_top
        tops[step, 1:2, :] = s_top
        t_new = jnp.maximum(run[0:1, :], t_top)
        s_new = jnp.maximum(run[3:4, :], s_top)
        t_old, t_add = jnp.exp(run[0:1, :] - t_new), jnp.exp(t_top - t_new)
        s_old, s_add = jnp.exp(run[3:4, :] - s_new), jnp.exp(s_top - s_new)
        t_sum = jnp.sum(t_exp, axis=0, keepdims=True)
        cross = jnp.sum(t_exp * (t - s), axis=0, keepdims=True)
        s_sum = jnp.sum(s_exp, axis=0, keepdims=True)
        run[1:2, :] = run[1:2, :] * t_old + t_sum * t_add
        run[2:3, :] = run[2:3, :] * t_old + cross * t_add
        run[4:5, :] = run[4:5, :] * s_old + s_sum * s_add
        run[0:1, :] = t_new
        run[3:4, :] = s_new

    by_block(step, vocab, block, multiply)
    if run is not None:

        @pl.when(step == steps - 1)
        def _():
            for dest in range(stats.shape[0]):
                stats[dest] = run[...]


def by_block(step, vocab, block, body):
    whole, tail = vocab // block, vocab % block
    if tail == 0:
        body(block)
        return
    if whole > 0:
        pl.when(step < whole)(functools.partial(body, block))
    pl.when(step == whole)(functools.partial(body, tail))


def stage(shards, picks, offs, wt, ws, held, dt, ds, copies=0):
    count, pieces = len(shards), len(shards[0])
    vocab = wt.shape[0]
    last = copies > 0
    rows = sum(part.shape[0] for part in shards[0])
    block = last_block if last else rows_per_block(vocab, 800)
    block = min(block, vocab)
    blocks = pl.cdiv(vocab, block)
    parts = [part for shard in shards for part in shard]
    in_specs = [WHOLE] * len(parts)
    for width in (dt, ds):
        in_specs += [
            pl.BlockSpec((block, width), lambda j, o, pick=pick: (j, o[pick])) for pick in picks
        ]
    args = [pinned(part) for part in parts] + [wt] * count + [ws] * count
    aliases = {}
    if held is not None:
        aliases = {1 + len(args): 0, 2 + len(args): 1}
        in_specs += [WHOLE, WHOLE]
        args += [pinned(array) for array in held]
    out_shape, out_specs = [pltpu.VMEM((vocab, rows), f32)] * 2, [WHOLE, WHOLE]
    scratch = []
    if last:
        for shape in ((blocks, 8, rows), (copies, 8, rows)):
            out_shape.append(jax.ShapeDtypeStruct(shape, f32))
            out_specs.append(WHOLE)
        scratch += [pltpu.VMEM((count, rows, width), bf16) for width in (dt, ds)]
        scratch.append(pltpu.VMEM((8, rows), f32))
    return pl.pallas_call(
        functools.partial(stage_kernel, count, pieces, dt, held is None, block),
        grid_spec=pltpu.PrefetchScalarGridSpec(
            num_scalar_prefetch=1,
            grid=(blocks,),
            in_specs=in_specs,
            out_specs=out_specs,
            scratch_shapes=scratch,
        ),
        out_shape=out_shape,
        input_output_aliases=aliases,
        compiler_params=pltpu.CompilerParams(vmem_limit_bytes=24 * MIB),
        cost_estimate=pl.CostEstimate(
            flops=2 * rows * count * (dt + ds) * vocab,
            bytes_accessed=2 * count * (dt + ds) * vocab,
            transcendentals=2 * rows * vocab if last else 0,
        ),
        name="stage_last" if last else "stage",
    )(offs, *args)


def grad_kernel(block, off_ref, stats, tops, t_exp, s_exp, ws, kl, own, other, total, lse):
    step = pl.program_id(0)
    vocab, rows = t_exp.shape
    half = rows // 2

    @pl.when(step == 0)
    def _():
        me = off_ref[off_ref.shape[0] - 1]
        sides = []
        for chip in range(stats.shape[0] // 2):
            sides.append(stats[2 * chip + me])
            mate = stats[2 * chip + 1 - me]
            sides.append(jnp.concatenate([mate[:, half:], mate[:, :half]], axis=1))
        t_top = functools.reduce(jnp.maximum, [side[0:1] for side in sides])
        s_top = functools.reduce(jnp.maximum, [side[3:4] for side in sides])
        t_sum = sum(side[1:2] * jnp.exp(side[0:1] - t_top) for side in sides)
        cross = sum(side[2:3] * jnp.exp(side[0:1] - t_top) for side in sides)
        s_sum = sum(side[4:5] * jnp.exp(side[3:4] - s_top) for side in sides)
        t_lse = t_top + jnp.log(t_sum)
        s_lse = s_top + jnp.log(s_sum)
        lse[0:1, :] = t_lse
        lse[1:2, :] = s_lse
        kl[...] = cross / t_sum - t_lse + s_lse
        total[...] = jnp.zeros_like(total)

    def add(size):
        here = pl.ds(pl.multiple_of(step * block, 8), size)
        t_scale = jnp.exp(tops[step, 0:1, :] - lse[0:1, :])
        s_scale = jnp.exp(tops[step, 1:2, :] - lse[1:2, :])
        grad = (s_exp[here, :] * s_scale - t_exp[here, :] * t_scale).astype(bf16)
        total[...] += lax.dot_general(grad, ws[:size], TN, preferred_element_type=f32)

    by_block(step, vocab, block, add)

    @pl.when(step == pl.num_programs(0) - 1)
    def _():
        width = own.shape[2]
        for dest in range(own.shape[0]):
            own[dest] = total[:half, dest * width : (dest + 1) * width]
            other[dest] = total[half:, dest * width : (dest + 1) * width].astype(bf16)


def grad_partial(offs, stats, tops, t_exp, s_exp, ws, count):
    vocab, rows = t_exp.shape
    features = ws.shape[1]
    block = min(last_block, vocab)
    shares = (count, rows // 2, features // count)

    return pl.pallas_call(
        functools.partial(grad_kernel, block),
        grid_spec=pltpu.PrefetchScalarGridSpec(
            num_scalar_prefetch=1,
            grid=(pl.cdiv(vocab, block),),
            in_specs=[
                WHOLE,
                WHOLE,
                WHOLE,
                WHOLE,
                pl.BlockSpec((block, features), lambda j, o: (j, 0)),
            ],
            out_specs=[WHOLE, WHOLE, WHOLE],
            scratch_shapes=[pltpu.VMEM((rows, features), f32), pltpu.VMEM((8, rows), f32)],
        ),
        out_shape=[
            jax.ShapeDtypeStruct((1, rows), f32),
            jax.ShapeDtypeStruct(shares, f32),
            jax.ShapeDtypeStruct(shares, bf16),
        ],
        compiler_params=pltpu.CompilerParams(vmem_limit_bytes=24 * MIB),
        cost_estimate=pl.CostEstimate(
            flops=2 * rows * features * vocab,
            bytes_accessed=2 * features * vocab,
            transcendentals=0,
        ),
        name="grad",
    )(offs, stats, tops, pinned(t_exp), pinned(s_exp), ws)


def ring_order(count):
    return list(range(0, count, 2)) + list(range(count - 1, 0, -2))


def ringed(teacher_hidden, teacher_weight, student_hidden, student_weight, loss_mask):
    count = lax.axis_size("vocab")
    dt, ds = teacher_hidden.shape[1], student_hidden.shape[1]
    order = ring_order(count)
    place = {device: at for at, device in enumerate(order)}
    table = [[order[(place[d] + k) % count] for k in range(count)] for d in range(count)]
    offs = lax.dynamic_index_in_dim(
        jnp.array(table, jnp.int32), lax.axis_index("vocab"), 0, False
    )
    offs = jnp.concatenate([offs, lax.axis_index("tok").astype(jnp.int32)[None]])
    up = [(order[i], order[(i + 1) % count]) for i in range(count)]
    down = [(b, a) for a, b in up]

    def sibling(array):
        return lax.ppermute(array, "tok", SWAP)

    wide = ((0, 0, 0), (0, ds, 0)), ((0, 0, 0), (dt, 0, 0))
    nothing = jnp.zeros((), teacher_hidden.dtype)
    mine = jnp.where(
        lax.broadcasted_iota(jnp.int32, (teacher_hidden.shape[0], dt + ds), 1) < dt,
        lax.pad(teacher_hidden, nothing, wide[0]),
        lax.pad(student_hidden, nothing, wide[1]),
    )
    half = mine.shape[0] // 2
    wt, ws = teacher_weight.T, student_weight.T
    from_low = from_high = mine
    run = functools.partial(stage, offs=offs, wt=wt, ws=ws, dt=dt, ds=ds)
    held, waiting, picks = None, [(mine, sibling(mine))], (0,)
    for hop in range(1, count // 2 + 1):
        final = hop == count // 2
        next_low = lax.ppermute(from_low[:half] if final else from_low, "vocab", up)
        next_high = lax.ppermute(from_high[half:] if final else from_high, "vocab", down)
        held = run(waiting, picks, held=held)
        from_low, from_high, *held = lax.optimization_barrier((next_low, next_high, *held))
        if final:
            waiting = [(from_low, from_high, sibling(from_low), sibling(from_high))]
            picks = (hop,)
        else:
            waiting = [(from_low, sibling(from_low)), (from_high, sibling(from_high))]
            picks = (count - hop, hop)
    t_exp, s_exp, tops, stats = run(waiting, picks, held=held, copies=2 * count)
    every = lax.all_to_all(stats, ("vocab", "tok"), 0, 0, tiled=True)
    kl, own, other = grad_partial(offs, every, tops, t_exp, s_exp, ws, count)
    rows = teacher_hidden.shape[0]
    beside = sibling(other)
    partial = (own + beside.astype(f32)).astype(bf16)
    chip, units = lax.axis_index("vocab"), count // 2
    middle = units // 2

    def goal(c, shift, flip):
        return (c // 2 + shift) % units * 2 + (c % 2 + flip) % 2

    def share(shift, flip):
        return lax.dynamic_index_in_dim(partial, goal(chip, shift, flip), 0, False)

    def exact(shift, flip):
        at = goal(chip, shift, flip)
        pair = [lax.dynamic_index_in_dim(array, at, 0, False) for array in (own, beside)]
        return pair[0] + pair[1].astype(f32)

    def sent(value, shift, flip):
        return lax.ppermute(value, "vocab", [(c, goal(c, shift, flip)) for c in range(count)])

    near = sent(jnp.stack([share(0, 1), share(middle, 1)]), 0, 1).astype(f32)
    total = exact(0, 0) + near[0]
    for shift in range(1, units):
        if shift != middle:
            for flip in range(2):
                total = total + sent(share(shift, flip), shift, flip).astype(f32)
    merged = (exact(middle, 0) + near[1]).astype(bf16)
    total = total + sent(merged, middle, 0).astype(f32)
    mask = loss_scale * loss_mask.astype(f32)
    return (kl[0, :rows], (mask[:, None] * total).astype(bf16))


def gathered(teacher_hidden, teacher_weight, student_hidden, student_weight, loss_mask):
    axes = ("vocab", "tok")

    def every_row(hidden):
        own = lax.all_gather(hidden, "vocab", axis=1, tiled=True)
        return lax.all_gather(own, "tok", axis=0, tiled=True)

    t = jnp.dot(every_row(teacher_hidden), teacher_weight, preferred_element_type=f32)
    s = jnp.dot(every_row(student_hidden), student_weight, preferred_element_type=f32)

    def log_total(logits):
        top = lax.pmax(jnp.max(logits, axis=1), axes)
        return top + jnp.log(lax.psum(jnp.sum(jnp.exp(logits - top[:, None]), axis=1), axes))

    t_log = t - log_total(t)[:, None]
    s_log = s - log_total(s)[:, None]
    teacher = jnp.exp(t_log)
    kl = lax.psum(jnp.sum(teacher * (t_log - s_log), axis=1), axes)
    grad = (jnp.exp(s_log) - teacher).astype(bf16)
    part = lax.dot_general(grad, student_weight, NT, preferred_element_type=f32)
    part = lax.psum_scatter(part, "tok", scatter_dimension=0, tiled=True)
    part = lax.psum_scatter(part, "vocab", scatter_dimension=1, tiled=True)
    rows = teacher_hidden.shape[0]
    mask = loss_scale * loss_mask.astype(f32)
    kl = lax.dynamic_slice_in_dim(kl, lax.axis_index("tok") * rows, rows)
    return (kl, (mask[:, None] * part).astype(bf16))


def shards(teacher_hidden, teacher_weight, student_hidden, student_weight, loss_mask):
    count = lax.axis_size("vocab")
    lanes = teacher_hidden.shape[1] % 128 == 0 and student_hidden.shape[1] % 128 == 0
    rows = teacher_hidden.shape[0] % 32 == 0 and teacher_weight.shape[1] % 16 == 0
    fits = lanes and rows and count % 2 == 0 and count >= 4 and lax.axis_size("tok") == 2
    run = ringed if fits else gathered
    return run(teacher_hidden, teacher_weight, student_hidden, student_weight, loss_mask)


def solution(mesh):
    return jax.shard_map(
        shards,
        mesh=mesh,
        in_specs=(
            P(("groups", "tok"), "vocab"),
            P(None, ("vocab", "tok")),
            P(("groups", "tok"), "vocab"),
            P(None, ("vocab", "tok")),
            P(("groups", "tok")),
        ),
        out_specs=(P(("groups", "tok")), P(("groups", "tok"), "vocab")),
        check_vma=False,
    )
```
